32 devices in a mesh: bond: 8 (over z, x), sector: 4 (over y, core).
Axes of the slice: x: 2, y: 2, z: 4, core: 2. Of those that a mesh axis runs over, the one named last changes fastest.
Arguments:
- theta: bfloat16 [4, 768, 768], P('sector'), may hold values from -80 to 80
- sector_dims: int32 [4], P('sector'), may hold values from 1 to 768, 2304 in all
- right_dims: int32 [4], P('sector'), may hold values from 1 to 768, 2304 in all
- env_left: bfloat16 [16, 4, 768, 768], P('bond', 'sector'), may hold values from -0.21875 to 0.21875
- env_right: bfloat16 [16, 4, 768, 768], P('bond', 'sector'), may hold values from -0.21875 to 0.21875
- mpo_on: int32 [16], P('bond'), may hold values 0 or 1
- mpo_coef: float32 [16], P('bond'), may hold values from -3 to 3
- mix_index: int32 [16, 3], P('bond'), may hold values from 0 to 7
- weight_table: float32 [8], replicated, may hold values from -3 to 3
Outputs:
- matvec: bfloat16 [4, 768, 768], P('sector', 'bond')
- env_next: bfloat16 [16, 4, 768, 768], P('bond', 'sector')
The draws below stay inside these ranges and needn't reach their ends.
All inputs are finite; a program needn't handle non-finite values. No bound on the sum of `sector_dims` or of `right_dims` or of `mpo_on` on one device may be relied on, other than what follows from the above.
Results may differ from the reference program's by a relative error of at most 0.008.
Values may be sent and summed in bfloat16 or wider, within the bound.
No kernel may reach another device: no remote copies, remote signals or barrier semaphores. Data moves between devices by JAX's collectives and lax.ppermute only.
A program may use at most 64 MiB of HBM per device.

```python
import math
import jax
import jax.numpy as jnp
import numpy as np
from jax import lax

DS = 768
NW = 8
BOND = 16
NSEC = 4


def draw_theta(key, part):
    key_base, key_row, key_col = jax.random.split(key, 3)
    sector_pos = jnp.arange(NSEC, dtype=jnp.float32) / max(NSEC - 1, 1)
    sector_scale = jnp.sqrt(1.0 + 2.0 * sector_pos)[:, None, None]
    base = jnp.clip(jax.random.normal(key_base, (NSEC, DS, DS), jnp.float32), -4.0, 4.0)
    row_scale = jnp.exp(jax.random.uniform(key_row, (NSEC, DS, 1), jnp.float32, math.log(0.3), math.log(3.0)))
    col_scale = jnp.exp(jax.random.uniform(key_col, (NSEC, 1, DS), jnp.float32, math.log(0.3), math.log(3.0)))
    return (base * row_scale * col_scale * sector_scale).astype(jnp.bfloat16)


def touch_ends(result, key, smallest, largest):
    place = [jax.random.randint(jax.random.fold_in(key, axis), (), 0, length) for axis, length in enumerate(result.shape)]
    longest = result.shape.index(max(result.shape))
    next_to = place[:longest] + [(place[longest] + 1) % result.shape[longest]] + place[longest + 1:]
    return result.at[tuple(place)].set(smallest).at[tuple(next_to)].set(largest)


def block_scale(key, dims, pieces, low, largest):
    loudness, own = 1.0, jax.random.fold_in(key, 6)
    for axis_at, blocks in pieces:
        draws = jnp.exp(jax.random.uniform(jax.random.fold_in(own, axis_at), (blocks,), jnp.float32, low / len(pieces), largest / len(pieces)))
        loudness = loudness * jnp.repeat(draws, dims[axis_at] // blocks).reshape([-1 if axis == axis_at else 1 for axis in range(len(dims))])
    return loudness


def profile(count, total, reach, skew):
    weights = [(1 << 20) // math.isqrt(standing ** skew) + 1 for standing in range(2, count + 1)]
    surplus, given = total - reach - (count - 1), [1] * (count - 1)
    while surplus > 0:
        candidates = [i for i in range(count - 1) if given[i] < reach]
        whole, left = sum([weights[i] for i in candidates]), surplus
        for i in candidates:
            extra = min(reach - given[i], max(1, left * weights[i] // whole), surplus)
            given[i] = given[i] + extra
            surplus = surplus - extra
    return np.array([reach] + given)


def ragged(own_key, count, total, reach, lean):
    if count == 2:
        one = jax.random.randint(own_key, (), max(1, total - reach), min(reach, total - 1) + 1)
        return jnp.stack([one, total - one])
    lengths = jnp.asarray(profile(count, total, reach, lean), jnp.int32)
    pairs = (count - 1) // 2
    giver, sink = lengths[1:1 + 2 * pairs:2], lengths[2:2 + 2 * pairs:2]
    margin = jnp.minimum(giver - 1, reach - sink)
    moved = jax.random.randint(jax.random.fold_in(own_key, 1), (pairs,), 0, 1 << 20) % (margin + 1)
    lengths = lengths.at[1:1 + 2 * pairs:2].set(giver - moved).at[2:2 + 2 * pairs:2].set(sink + moved)
    return lengths[jax.random.permutation(jax.random.fold_in(own_key, 2), count)]


def bell_draw(key, extent, spread, limit, shards=(), held_as=jnp.bfloat16):
    level = block_scale(key, extent, shards, -0.22, 0.18) if shards else 1.0
    entries = jax.random.normal(key, extent, jnp.float32) * spread * level
    return jnp.minimum(jnp.maximum(entries, -limit), limit).astype(held_as)


def setup_inputs(seed: int = 0) -> dict:
    arg_keys = jax.random.split(jax.random.key(seed), 10)
    theta = draw_theta(jax.random.fold_in(arg_keys[9], 71), 0)
    sector_dims = ragged(arg_keys[1], NSEC, NSEC * DS * 3 // 4, DS, 1).astype(jnp.int32)
    right_dims = ragged(arg_keys[2], NSEC, NSEC * DS * 3 // 4, DS, 1).astype(jnp.int32)
    env_left = bell_draw(arg_keys[3], (BOND, NSEC, DS, DS), DS ** -0.5, 0.21875, ((0, 8), (1, 4)))
    env_right = bell_draw(arg_keys[4], (BOND, NSEC, DS, DS), DS ** -0.5, 0.21875, ((0, 8), (1, 4)))
    mpo_on = touch_ends((jax.random.randint(arg_keys[5], (BOND,), 0, 4) < 3).astype(jnp.int32), jax.random.fold_in(arg_keys[5], 1), 0, 1)
    mpo_coef = bell_draw(arg_keys[6], (BOND,), 0.3, 3.0, ((0, 8),), jnp.float32)
    mix_index = touch_ends(jax.random.randint(arg_keys[7], (BOND, 3), 0, NW), jax.random.fold_in(arg_keys[7], 1), 0, NW - 1).astype(jnp.int32)
    weight_table = bell_draw(arg_keys[8], (NW,), 0.6, 3.0, (), jnp.float32)
    return dict(theta=theta, sector_dims=sector_dims, right_dims=right_dims, env_left=env_left, env_right=env_right, mpo_on=mpo_on, mpo_coef=mpo_coef, mix_index=mix_index, weight_table=weight_table)


def reference(theta, sector_dims, right_dims, env_left, env_right, mpo_on, mpo_coef, mix_index, weight_table):
    index = jnp.arange(DS, dtype=jnp.int32)
    row_live = (index[None, :] < sector_dims[:, None]).astype(jnp.float32)
    col_live = (index[None, :] < right_dims[:, None]).astype(jnp.float32)
    block_mask = row_live[:, :, None] * col_live[:, None, :]
    live = (theta.astype(jnp.float32) * block_mask).astype(jnp.bfloat16)
    gain = mpo_coef * mpo_on.astype(jnp.float32)
    mix_gain = weight_table[mix_index]
    left_moved = jnp.moveaxis(env_left, 1, 0)
    right_moved = jnp.moveaxis(env_right, 1, 0)

    def sector_matvec(items):
        live_block, left_block, right_block, mask_block = items
        applied = jnp.einsum('wab,bc->wac', left_block.astype(jnp.float32), live_block.astype(jnp.float32)).astype(jnp.bfloat16)
        terms = jnp.einsum('wac,wdc->wad', applied.astype(jnp.float32), right_block.astype(jnp.float32))
        return mask_block * jnp.einsum('w,wad->ad', gain, terms)
    product_sum = lax.map(sector_matvec, (live, left_moved, right_moved, block_mask))
    matvec = product_sum.astype(jnp.bfloat16)
    square_total = jnp.sum(product_sum * product_sum)
    unit = (product_sum * lax.rsqrt(square_total / (NSEC * DS * DS) + 1e-06)).astype(jnp.bfloat16)

    def sector_grow(items):
        unit_block, left_block = items
        zero = jnp.zeros((1, DS, DS), jnp.bfloat16)
        padded = jnp.concatenate([zero, left_block, zero], axis=0).astype(jnp.float32)
        mixed = (mix_gain[:, 0, None, None] * padded[:-2] + mix_gain[:, 1, None, None] * padded[1:-1] + mix_gain[:, 2, None, None] * padded[2:]).astype(jnp.bfloat16)
        half = jnp.einsum('wab,bc->wac', mixed.astype(jnp.float32), unit_block.astype(jnp.float32)).astype(jnp.bfloat16)
        grown = jnp.einsum('ba,wbc->wac', unit_block.astype(jnp.float32), half.astype(jnp.float32))
        return (grown / math.sqrt(DS)).astype(jnp.bfloat16)
    grown_all = lax.map(sector_grow, (unit, left_moved))
    env_next = jnp.moveaxis(grown_all, 0, 1)
    return (matvec, env_next)
```

```python
import functools
import math

import jax
import jax.numpy as jnp
from jax import lax
from jax.experimental import pallas as pl
from jax.experimental.pallas import tpu as pltpu
from jax.sharding import PartitionSpec as P

F32, BF16 = jnp.float32, jnp.bfloat16
SMEM = pl.BlockSpec(memory_space=pltpu.SMEM)
VMEM = pl.BlockSpec(memory_space=pltpu.VMEM)
NT = (((1,), (1,)), ((), ()))
TN = (((0,), (0,)), ((), ()))


def strip_of(states):
    return 256 if states % 256 == 0 else states


def partial_kernel(
    outer, inner, rows_ref, cols_ref, on_ref, coef_ref, theta_ref, left_ref, right_ref, out_ref, live, acc
):
    channel, last = pl.program_id(0), pl.num_programs(0) - 1
    states = theta_ref.shape[-1]
    share, strip = states // (outer * inner), strip_of(states)

    @pl.when(channel == 0)
    def _():
        row = lax.broadcasted_iota(jnp.int32, (states, states), 0)
        col = lax.broadcasted_iota(jnp.int32, (states, states), 1)
        keep = (row < rows_ref[0]) & (col < cols_ref[0])
        theta = theta_ref[0].astype(F32)
        live[...] = jnp.where(keep, theta, 0.0).astype(BF16)
        acc[...] = jnp.zeros_like(acc)

    gain = coef_ref[channel] * on_ref[channel].astype(F32)
    for at in range(0, states, strip):
        here = pl.ds(at, strip)
        applied = jnp.dot(left_ref[0, 0, here, :], live[...], preferred_element_type=F32).astype(BF16)
        term = lax.dot_general(applied, right_ref[0, 0], NT, preferred_element_type=F32)
        acc[here, :] += gain * term

    @pl.when(channel == last)
    def _():
        for hi in range(outer):
            for lo in range(inner):
                block = acc[pl.ds((hi * inner + lo) * share, share), :]
                out_ref[lo, pl.ds(hi * share, share), :] = block.astype(BF16)


def partial_sums(outer, inner, rows, cols, on, coef, theta, left, right):
    channels, states = left.shape[0], theta.shape[-1]
    block = pl.BlockSpec((1, 1, states, states), lambda c: (c, 0, 0, 0))
    whole = pl.BlockSpec((1, states, states), lambda c: (0, 0, 0))
    return pl.pallas_call(
        functools.partial(partial_kernel, outer, inner),
        name="partial_sums",
        grid=(channels,),
        out_shape=jax.ShapeDtypeStruct((inner, states // inner, states), BF16),
        in_specs=[SMEM, SMEM, SMEM, SMEM, whole, block, block],
        out_specs=pl.BlockSpec((inner, states // inner, states), lambda c: (0, 0, 0)),
        scratch_shapes=[pltpu.VMEM((states, states), BF16), pltpu.VMEM((states, states), F32)],
        cost_estimate=pl.CostEstimate(
            flops=4 * channels * states**3, bytes_accessed=4 * (channels + 1) * states**2, transcendentals=0
        ),
    )(rows, cols, on, coef, theta, left, right)


def grow_kernel(outer, inner, index_ref, table_ref, scale_ref, product_ref, own_ref, before_ref, after_ref, out_ref, unit, half):
    channels, states = own_ref.shape[0], own_ref.shape[-1]
    share, strip = states // (outer * inner), strip_of(states)
    scale = scale_ref[0]
    for hi in range(outer):
        for lo in range(inner):
            unit[pl.ds((hi * inner + lo) * share, share), :] = product_ref[lo, pl.ds(hi * share, share), :]
    around = [before_ref] + [own_ref.at[c, 0] for c in range(channels)] + [after_ref]
    for c in range(channels):
        for at in range(0, states, strip):
            here = pl.ds(at, strip)
            mixed = sum(
                table_ref[index_ref[c, k]] * around[c + k][here, :].astype(F32) for k in range(3)
            ).astype(BF16)
            first = jnp.dot(mixed, unit[...], preferred_element_type=F32)
            half[here, :] = (scale * first).astype(BF16)
        for at in range(0, states, strip):
            here = pl.ds(at, strip)
            second = lax.dot_general(unit[:, here], half[...], TN, preferred_element_type=F32)
            out_ref[c, 0, here, :] = (second * (scale * (1 / math.sqrt(states)))).astype(BF16)


def grow(outer, inner, index, table, scale, product, own, before, after):
    channels, states = own.shape[0], own.shape[-1]
    return pl.pallas_call(
        functools.partial(grow_kernel, outer, inner),
        name="grow",
        out_shape=jax.ShapeDtypeStruct(own.shape, BF16),
        in_specs=[SMEM, SMEM, SMEM, VMEM, VMEM, VMEM, VMEM],
        out_specs=VMEM,
        scratch_shapes=[pltpu.VMEM((states, states), BF16), pltpu.VMEM((states, states), BF16)],
        cost_estimate=pl.CostEstimate(
            flops=4 * channels * states**3, bytes_accessed=4 * (channels + 2) * states**2, transcendentals=0
        ),
    )(index, table, scale, product, own, before, after)


def rims(shard, axis):
    peers, length = lax.axis_size(axis), shard.shape[0]
    up = [(i, i + 1) for i in range(peers - 1)]
    down = [(j, i) for i, j in up]
    return lax.ppermute(shard[length - 1], axis, up), lax.ppermute(shard[0], axis, down)


def everyone(value, axes):
    for axis in axes:
        peers = lax.axis_size(axis)
        if peers & (peers - 1):
            value = lax.psum(value, axis)
            continue
        for bit in range(peers.bit_length() - 1):
            value = value + lax.ppermute(value, axis, [(i, i ^ (1 << bit)) for i in range(peers)])
    return value


def on_device(
    theta, sector_dims, right_dims, env_left, env_right, mpo_on, mpo_coef, mix_index, weight_table
):
  states = theta.shape[1]
  bonds, sectors = lax.axis_size("bond"), lax.axis_size("sector")
  share = states // bonds
  before, after = rims(env_left[:, 0], "bond")
  first = lax.axis_index("bond") * share
  count_all = sectors * states * states
  parts = partial_sums(bonds, 1, sector_dims, right_dims, mpo_on, mpo_coef, theta, env_left, env_right)
  met = lax.all_to_all(parts.reshape(bonds, share, states), "bond", 0, 0, tiled=True)
  rows = jnp.sum(met.astype(F32), axis=0)
  row_ids = first + jnp.arange(share, dtype=jnp.int32)
  keep = (row_ids < sector_dims[0])[:, None] & (jnp.arange(states, dtype=jnp.int32) < right_dims[0])[None, :]
  rows = jnp.where(keep, rows, 0.0)
  matvec = rows.astype(BF16)
  product = lax.all_to_all(jnp.broadcast_to(matvec[None], (bonds, share, states)), "bond", 0, 0, tiled=True)
  square_total = everyone(jnp.broadcast_to(jnp.sum(rows * rows), (1, 128)), ("sector", "bond"))[0, 0]
  scale = lax.rsqrt(square_total / count_all + 1e-06)
  grown = grow(bonds, 1, mix_index, weight_table, scale.reshape(1), product.reshape(1, states, states), env_left, before, after)
  return matvec[None], grown


def solution(mesh):
    in_specs = (
        P("sector", None, None),
        P("sector"),
        P("sector"),
        P("bond", "sector", None, None),
        P("bond", "sector", None, None),
        P("bond"),
        P("bond"),
        P("bond", None),
        P(),
    )
    out_specs = (P("sector", "bond", None), P("bond", "sector", None, None))
    return jax.shard_map(
        on_device, mesh=mesh, in_specs=in_specs, out_specs=out_specs, check_vma=False
    )
```

```python
import functools
import math

import jax
import jax.numpy as jnp
from jax import lax
from jax.experimental import pallas as pl
from jax.experimental.pallas import tpu as pltpu
from jax.sharding import PartitionSpec as P

F32, BF16 = jnp.float32, jnp.bfloat16
SMEM = pl.BlockSpec(memory_space=pltpu.SMEM)
VMEM = pl.BlockSpec(memory_space=pltpu.VMEM)
NT = (((1,), (1,)), ((), ()))


def strip_of(states):
    return 256 if states % 256 == 0 else states


def partial_kernel(
    outer, inner, rows_ref, cols_ref, on_ref, coef_ref, theta_ref, left_ref, right_ref, out_ref, live, acc
):
    channel, last = pl.program_id(0), pl.num_programs(0) - 1
    states = theta_ref.shape[-1]
    share, strip = states // (outer * inner), strip_of(states)

    @pl.when(channel == 0)
    def _():
        row = lax.broadcasted_iota(jnp.int32, (states, states), 0)
        col = lax.broadcasted_iota(jnp.int32, (states, states), 1)
        keep = (row < rows_ref[0]) & (col < cols_ref[0])
        theta = theta_ref[0].astype(F32)
        live[...] = jnp.where(keep, theta, 0.0).astype(BF16)
        acc[...] = jnp.zeros_like(acc)

    gain = coef_ref[channel] * on_ref[channel].astype(F32)
    for at in range(0, states, strip):
        here = pl.ds(at, strip)
        applied = jnp.dot(left_ref[0, 0, here, :], live[...], preferred_element_type=F32).astype(BF16)
        term = lax.dot_general(applied, right_ref[0, 0], NT, preferred_element_type=F32)
        acc[here, :] += gain * term

    @pl.when(channel == last)
    def _():
        for hi in range(outer):
            for lo in range(inner):
                block = acc[pl.ds((hi * inner + lo) * share, share), :]
                out_ref[lo, pl.ds(hi * share, share), :] = block.astype(BF16)


def partial_sums(outer, inner, rows, cols, on, coef, theta, left, right):
    channels, states = left.shape[0], theta.shape[-1]
    block = pl.BlockSpec((1, 1, states, states), lambda c: (c, 0, 0, 0))
    whole = pl.BlockSpec((1, states, states), lambda c: (0, 0, 0))
    return pl.pallas_call(
        functools.partial(partial_kernel, outer, inner),
        name="partial_sums",
        grid=(channels,),
        out_shape=jax.ShapeDtypeStruct((inner, states // inner, states), BF16),
        in_specs=[SMEM, SMEM, SMEM, SMEM, whole, block, block],
        out_specs=pl.BlockSpec((inner, states // inner, states), lambda c: (0, 0, 0)),
        scratch_shapes=[pltpu.VMEM((states, states), BF16), pltpu.VMEM((states, states), F32)],
        cost_estimate=pl.CostEstimate(
            flops=4 * channels * states**3, bytes_accessed=4 * (channels + 1) * states**2, transcendentals=0
        ),
    )(rows, cols, on, coef, theta, left, right)


LIFT = 2.0**40


def end_of(parity, channels, far):
    return jnp.where(far == 1, parity, 1 - parity) * (channels - 1)


def mix_rows(me_ref, index_ref, table_ref, own_ref, edges, mixed):
    far, parity, channels = pl.program_id(0), lax.rem(me_ref[0], 2), own_ref.shape[0]
    channel = end_of(parity, channels, far)
    step = (2 * far - 1) * (1 - 2 * parity)
    outward, centre, inward = (table_ref[index_ref[channel, k]] for k in (1 - step, 1, 1 + step))

    def mix(edge_ref):
        total = centre * own_ref[channel, 0].astype(F32) + inward * own_ref[channel + step, 0].astype(F32)
        mixed[...] = (total + outward * edge_ref[...].astype(F32)).astype(BF16)

    @pl.when(far == 0)
    def _():
        mix(edges[0])

    @pl.when(far == 1)
    def _():
        mix(edges[1])


def premix_kernel(me_ref, index_ref, table_ref, own_ref, near_ref, far_ref, out_ref):
    mix_rows(me_ref, index_ref, table_ref, own_ref, (near_ref, far_ref), out_ref.at[0])


def premix(me, index, table, own, near, far):
    channels, states, rows = own.shape[0], own.shape[-1], near.shape[0]
    edge = pl.BlockSpec((rows, states), lambda g: (0, 0))
    return pl.pallas_call(
        premix_kernel,
        name="premix",
        out_shape=jax.ShapeDtypeStruct((2, rows, states), BF16),
        grid=(2,),
        in_specs=[SMEM] * 3 + [pl.BlockSpec((channels, 1, rows, states), lambda g: (0, 0, 0, 0)), edge, edge],
        out_specs=pl.BlockSpec((1, rows, states), lambda g: (g, 0, 0)),
        cost_estimate=pl.CostEstimate(flops=12 * rows * states, bytes_accessed=12 * rows * states, transcendentals=0),
    )(me, index, table, own, near, far)


def turn_kernel(product_ref, turned_ref, square_ref):
    product = product_ref[...]
    wide = product.astype(F32)
    total = jnp.sum(jnp.sum(wide * wide, axis=0, keepdims=True), axis=1, keepdims=True)
    square_ref[...] = jnp.broadcast_to(total, square_ref.shape)
    turned_ref[...] = product.T


def turn(product):
    states = product.shape[-1]
    return pl.pallas_call(
        turn_kernel,
        name="turn",
        out_shape=[jax.ShapeDtypeStruct(product.shape, BF16), jax.ShapeDtypeStruct((8, 128), F32)],
        in_specs=[VMEM],
        out_specs=[VMEM, VMEM],
        cost_estimate=pl.CostEstimate(flops=2 * states**2, bytes_accessed=4 * states**2, transcendentals=0),
    )(product)


def early_kernel(product_ref, mixed_ref, out_ref):
    for g in range(2):
        first = jnp.dot(mixed_ref[g], product_ref[...], preferred_element_type=F32)
        out_ref[g] = (LIFT * first).astype(BF16)


def early(product, mixed):
    return pl.pallas_call(
        early_kernel,
        name="early",
        out_shape=jax.ShapeDtypeStruct(mixed.shape, BF16),
        in_specs=[VMEM, VMEM],
        out_specs=VMEM,
        cost_estimate=pl.CostEstimate(flops=2 * mixed.size * product.shape[0], bytes_accessed=6 * mixed.size, transcendentals=0),
    )(product, mixed)


def late_kernel(
    me_ref, index_ref, table_ref, scale_ref, product_ref, turned_ref, own_ref, early_ref, near_ref, far_ref, out_ref, mixed, half
):
    states, rows = product_ref.shape[-1], early_ref.shape[1]
    half[pl.ds(0, rows), :] = early_ref[0]
    mix_rows(me_ref, index_ref, table_ref, own_ref, (near_ref, far_ref), mixed)
    first = jnp.dot(mixed[...], product_ref[...], preferred_element_type=F32)
    half[pl.ds(rows, rows), :] = (LIFT * first).astype(BF16)
    factor = scale_ref[0] * scale_ref[0] * (1 / (LIFT * math.sqrt(states)))
    second = jnp.dot(turned_ref[...], half[...], preferred_element_type=F32)
    out_ref[0, 0] = (second * factor).astype(BF16)


def late(me, index, table, scale, product, turned, own, begun, near, far):
    channels, states, rows = own.shape[0], own.shape[-1], near.shape[0]
    edge = pl.BlockSpec((rows, states), lambda g, m: (0, 0))
    whole = pl.BlockSpec((states, states), lambda g, m: (0, 0))
    return pl.pallas_call(
        late_kernel,
        name="late",
        out_shape=jax.ShapeDtypeStruct(own.shape, BF16),
        grid_spec=pltpu.PrefetchScalarGridSpec(
            num_scalar_prefetch=1,
            grid=(2,),
            in_specs=[SMEM] * 3
            + [
                whole,
                whole,
                pl.BlockSpec((channels, 1, rows, states), lambda g, m: (0, 0, 1, 0)),
                pl.BlockSpec((1, rows, states), lambda g, m: (g, 0, 0)),
                edge,
                edge,
            ],
            out_specs=pl.BlockSpec(
                (1, 1, states, states), lambda g, m: (end_of(lax.rem(m[0], 2), channels, g), 0, 0, 0)
            ),
            scratch_shapes=[pltpu.VMEM((rows, states), BF16), pltpu.VMEM((states, states), BF16)],
        ),
        cost_estimate=pl.CostEstimate(flops=6 * states**3, bytes_accessed=16 * states**2, transcendentals=0),
    )(me, index, table, scale, product, turned, own, begun, near, far)


def everyone(value, axis):
    peers = lax.axis_size(axis)
    if peers & (peers - 1):
        return lax.psum(value, axis)
    terms = [value]
    for k in range(1, peers):
        terms.append(lax.ppermute(value, axis, [(i, i ^ k) for i in range(peers)]))
    while len(terms) > 1:
        terms = [a + b for a, b in zip(terms[::2], terms[1::2])]
    return terms[0]


def on_device(
    theta, sector_dims, right_dims, env_left, env_right, mpo_on, mpo_coef, mix_index, weight_table
):
    channels, states = env_left.shape[0], theta.shape[1]
    bonds, sectors = lax.axis_size("bond"), lax.axis_size("sector")
    share, cut = states // bonds, states // 2
    me = lax.axis_index("bond").astype(jnp.int32)
    pairs = {
        False: [(i, i ^ 1) for i in range(bonds) if i ^ 1 < bonds],
        True: [(i, (i + 1 ^ 1) - 1) for i in range(1, bonds) if (i + 1 ^ 1) - 1 < bonds],
    }

    def edge(source, far, at):
        end = end_of(me % 2, channels, int(far))
        slab = lax.dynamic_slice(source, (end, 0, at, 0), (1, 1, cut, states))[0, 0]
        return lax.ppermute(slab, "bond", pairs[far])

    near0 = edge(env_left, False, 0)
    far0 = edge(env_left, True, 0)
    parts = partial_sums(bonds, 1, sector_dims, right_dims, mpo_on, mpo_coef, theta, env_left, env_right)
    late_left, parts = lax.optimization_barrier((env_left, parts))
    met = lax.all_to_all(parts.reshape(bonds, share, states), "bond", 0, 0, tiled=True)
    near1 = edge(late_left, False, cut)
    far1 = edge(late_left, True, cut)
    rows = jnp.sum(met.astype(F32), axis=0)
    row_ids = me * share + jnp.arange(share, dtype=jnp.int32)
    keep = (row_ids < sector_dims[0])[:, None] & (jnp.arange(states, dtype=jnp.int32) < right_dims[0])[None, :]
    matvec = jnp.where(keep, rows, 0.0).astype(BF16)
    product = lax.all_to_all(jnp.broadcast_to(matvec[None], (bonds, share, states)), "bond", 0, 0, tiled=True)
    product = product.reshape(states, states)
    mixed = premix(jnp.reshape(me, (1,)), mix_index, weight_table, env_left, near0, far0)
    turned, square = turn(product)
    square_total = everyone(square, "sector")[0, 0]
    scale = lax.rsqrt(square_total / (sectors * states * states) + 1e-06).reshape(1)
    begun = early(product, mixed)
    grown = late(jnp.reshape(me, (1,)), mix_index, weight_table, scale, product, turned, env_left, begun, near1, far1)
    return matvec[None], grown


def solution(mesh):
    in_specs = (
        P("sector", None, None),
        P("sector"),
        P("sector"),
        P("bond", "sector", None, None),
        P("bond", "sector", None, None),
        P("bond"),
        P("bond"),
        P("bond", None),
        P(),
    )
    out_specs = (P("sector", "bond", None), P("bond", "sector", None, None))
    return jax.shard_map(
        on_device, mesh=mesh, in_specs=in_specs, out_specs=out_specs, check_vma=False
    )
```
